32 devices in a mesh: row: 8 (over z, y), col: 4 (over x, core).
Axes of the slice: x: 2, y: 2, z: 4, core: 2. Of those that a mesh axis runs over, the one named last changes fastest.
Arguments:
- tensor: bfloat16 [1024, 64, 512], P('row', None, 'col'), may hold values from -6 to 6
- loss_kind: int32 [1024, 64, 512], P('row', None, 'col'), may hold values from 0 to 1, as said below
- factor_one: float32 [1024, 512], P(('row', 'col')), may hold values from -2 to 2
- factor_two: float32 [512, 512], P(('col', 'row')), may hold values from -2 to 2
- factor_three: float32 [64, 512], replicated, may hold values from -2 to 2
- first_one: float32 [1024, 512], P(('row', 'col')), may hold values from -0.03 to 0.03
- second_one: float32 [1024, 512], P(('row', 'col')), may hold values from 0.0005 to 0.05
- first_two: float32 [512, 512], P(('col', 'row')), may hold values from -0.03 to 0.03
- second_two: float32 [512, 512], P(('col', 'row')), may hold values from 0.0005 to 0.05
- first_three: float32 [64, 512], replicated, may hold values from -0.03 to 0.03
- second_three: float32 [64, 512], replicated, may hold values from 0.0005 to 0.05
Outputs:
- new_one: float32 [1024, 512], P(('row', 'col'))
- new_two: float32 [512, 512], P(('col', 'row'))
- new_three: float32 [64, 512], replicated
The draws below stay inside these ranges and needn't reach their ends.
Inputs may be any that keep to these rules, and one draw needn't show every extreme that they name: loss_kind takes one value on each block of 128 first-mode by 128 second-mode indices (with all 64 third-mode ones), aligned to multiples of 128 and 128, and is 1 on exactly half of these blocks.
All inputs are finite; a program needn't handle non-finite values.
Results may differ from the reference program's by a relative error of at most 0.003.
Values may be sent and summed in bfloat16 or wider, within the bound.
A program may use at most 128 MiB of HBM per device.

```python
import math
import jax
import jax.numpy as jnp
from jax import lax

TI = 128
TJ = 128
K = 64
R = 512
ITERS = 2
STEP = 10
I = 1024
J = 512
N_ROW = 8


def draw_tensor(key, part):
    key_offset, key_gain, key_noise = jax.random.split(key, 3)
    row_blocks = I // TI
    col_blocks = J // TJ
    block_shape = (row_blocks, 1, 1, col_blocks, 1)
    full_shape = (row_blocks, TI, K, col_blocks, TJ)
    offset = jax.random.uniform(key_offset, block_shape, jnp.float32, -1.0, 1.0)
    gain = jnp.exp(jax.random.uniform(key_gain, block_shape, jnp.float32, -1.5, 0.7))
    noise = jax.random.normal(key_noise, full_shape, jnp.float32)
    values = jnp.clip(offset + gain * noise, -6.0, 6.0)
    return values.reshape(I, K, J).astype(jnp.bfloat16)


def draw_loss_kind(key, part):
    row_blocks = I // TI
    col_blocks = J // TJ
    order = jax.random.permutation(key, row_blocks * col_blocks)
    block_kind = (order % 2).astype(jnp.int32).reshape(row_blocks, 1, 1, col_blocks, 1)
    return jnp.broadcast_to(block_kind, (row_blocks, TI, K, col_blocks, TJ)).reshape(I, K, J)


def shard_levels(key, shape, pieces, smallest, high):
    factor_of = 1.0
    for dim, blocks in pieces:
        heights = jax.random.uniform(jax.random.fold_in(jax.random.fold_in(key, 6), dim), (blocks,), jnp.float32, smallest / len(pieces), high / len(pieces))
        factor_of = factor_of * jnp.repeat(jnp.exp(heights), shape[dim] // blocks).reshape((-1,) + (1,) * (len(shape) - 1 - dim))
    return factor_of


def bell_draw(rng, dims, deviation, most, cuts=(), held_as=jnp.bfloat16):
    level = shard_levels(rng, dims, cuts, -0.22, 0.18) if cuts else 1.0
    drawn = jax.random.normal(rng, dims, jnp.float32) * deviation * level
    return jnp.minimum(jnp.maximum(drawn, -most), most).astype(held_as)


def setup_inputs(seed: int = 0) -> dict:
    seeds = jax.random.split(jax.random.key(seed), 12)
    tensor = draw_tensor(jax.random.fold_in(seeds[11], 71), 0)
    loss_kind = draw_loss_kind(jax.random.fold_in(seeds[11], 71), 0)
    factor_one = bell_draw(seeds[2], (I, R), 0.35, 2.0, ((0, 32),), jnp.float32)
    factor_two = bell_draw(seeds[3], (J, R), 0.35, 2.0, ((0, 32),), jnp.float32)
    factor_three = bell_draw(seeds[4], (K, R), 0.35, 2.0, (), jnp.float32)
    first_one = bell_draw(seeds[5], (I, R), 0.005, 0.03, ((0, 32),), jnp.float32)
    second_one = jnp.clip(jnp.exp(math.log(0.05) - 4.6051702 * jax.random.uniform(seeds[6], (I, R), jnp.float32) ** shard_levels(seeds[6], (I, R), ((0, 32),), -0.2, 0.2)), 0.0005, 0.05)
    first_two = bell_draw(seeds[7], (J, R), 0.005, 0.03, ((0, 32),), jnp.float32)
    second_two = jnp.clip(jnp.exp(math.log(0.05) - 4.6051702 * jax.random.uniform(seeds[8], (J, R), jnp.float32) ** shard_levels(seeds[8], (J, R), ((0, 32),), -0.2, 0.2)), 0.0005, 0.05)
    first_three = bell_draw(seeds[9], (K, R), 0.005, 0.03, (), jnp.float32)
    second_three = jnp.clip(jnp.exp(jax.random.uniform(seeds[10], (K, R), jnp.float32, math.log(0.0005), math.log(0.05))), 0.0005, 0.05)
    return dict(tensor=tensor, loss_kind=loss_kind, factor_one=factor_one, factor_two=factor_two, factor_three=factor_three, first_one=first_one, second_one=second_one, first_two=first_two, second_two=second_two, first_three=first_three, second_three=second_three)


learn_rate = 0.05
beta_one = 0.8
beta_two = 0.95
adam_eps = 1e-08

def loss_slope(rebuilt, values, kinds):
    excess = rebuilt - values
    huber_part = jnp.clip(excess, -1.0, 1.0)
    target = jnp.where(values > 0, 1.0, 0.0).astype(rebuilt.dtype)
    logit_part = jax.nn.sigmoid(rebuilt) - target
    return jnp.where(kinds == 1, logit_part, huber_part)

def adam_step(param, first, second, grad, counter):
    first = beta_one * first + (1.0 - beta_one) * grad
    second = beta_two * second + (1.0 - beta_two) * grad * grad
    corr_one = 1.0 - beta_one ** counter
    corr_two = 1.0 - beta_two ** counter
    param = param - learn_rate * (first / corr_one) / (jnp.sqrt(second / corr_two) + adam_eps)
    return (param, first, second)

def all_grads(tensor, loss_kind, half_one, half_two, half_three):
    three_f = half_three.astype(jnp.float32)
    blocks = (tensor.reshape(N_ROW, TI, K, J), loss_kind.reshape(N_ROW, TI, K, J), half_one.reshape(N_ROW, TI, R))

    def block_step(carry, items):
        grad_two, grad_three = carry
        data_blk, kind_blk, one_blk = items
        one_f = one_blk.astype(jnp.float32)
        scaled_rows = (one_f[:, None, :] * three_f[None, :, :]).astype(jnp.bfloat16).reshape(TI * K, R)
        rebuilt = lax.dot_general(scaled_rows, half_two, (((1,), (1,)), ((), ())), preferred_element_type=jnp.float32)
        values = data_blk.reshape(TI * K, J).astype(jnp.float32)
        deriv_bf = loss_slope(rebuilt, values, kind_blk.reshape(TI * K, J)).astype(jnp.bfloat16)
        projected = jnp.dot(deriv_bf, half_two, preferred_element_type=jnp.float32).reshape(TI, K, R)
        grad_one = lax.optimization_barrier(jnp.sum(projected * three_f[None, :, :], axis=1))
        grad_three = grad_three + lax.optimization_barrier(jnp.sum(projected * one_f[:, None, :], axis=0))
        grad_two = grad_two + lax.dot_general(deriv_bf, scaled_rows, (((0,), (0,)), ((), ())), preferred_element_type=jnp.float32)
        return ((grad_two, grad_three), grad_one)
    start = (jnp.zeros((J, R), jnp.float32), jnp.zeros((K, R), jnp.float32))
    (grad_two, grad_three), grad_one = lax.scan(block_step, start, blocks)
    grad_one = grad_one.reshape(I, R) / math.sqrt(J * K)
    grad_two = grad_two / math.sqrt(I * K)
    grad_three = grad_three / math.sqrt(I * J)
    return (grad_one, grad_two, grad_three)

def reference(tensor, loss_kind, factor_one, factor_two, factor_three, first_one, second_one, first_two, second_two, first_three, second_three):
    start_one, start_two, start_three = (factor_one, factor_two, factor_three)
    for iteration in range(ITERS):
        grad_one, grad_two, grad_three = all_grads(tensor, loss_kind, factor_one.astype(jnp.bfloat16), factor_two.astype(jnp.bfloat16), factor_three.astype(jnp.bfloat16))
        counter = STEP + iteration + 1
        factor_one, first_one, second_one = adam_step(factor_one, first_one, second_one, grad_one, counter)
        factor_two, first_two, second_two = adam_step(factor_two, first_two, second_two, grad_two, counter)
        factor_three, first_three, second_three = adam_step(factor_three, first_three, second_three, grad_three, counter)
    spread = learn_rate * ITERS
    return ((start_one - factor_one) / spread, (start_two - factor_two) / spread, (start_three - factor_three) / spread)
```

```python
import functools
import math

import jax
import jax.numpy as jnp
from jax import lax
from jax.experimental import pallas as pl
from jax.experimental.pallas import tpu as pltpu
from jax.sharding import PartitionSpec as P

ITERS = 2
STEP = 10
BLOCK = 8
LANES = 128

learn_rate = 0.05
beta_one = 0.8
beta_two = 0.95
adam_eps = 1e-08

F32 = jnp.float32
BF16 = jnp.bfloat16


def adam_step(param, first, second, grad, counter):
    first = beta_one * first + (1.0 - beta_one) * grad
    second = beta_two * second + (1.0 - beta_two) * grad * grad
    corr_one = 1.0 - beta_one**counter
    corr_two = 1.0 - beta_two**counter
    param = param - learn_rate * (first / corr_one) / (jnp.sqrt(second / corr_two) + adam_eps)
    return (param, first, second)


def kernel(
    n_row, n_col, scales,
    tensor, kind, a_in, b_in, c_in, ma_in, va_in, mb_in, vb_in, mc_in, vc_in,
    oa, ob, oc,
    x_s, kind_s, ag_a, ag_b, ag_c, gs_a, gs_b, gs_c, rs_a, rs_b, rs_c,
    a_f, bt, c_f, ga, gb, gc, st_a, st_b, st_c, split,
    load_sem, sends, recvs,
):
    row = lax.axis_index("row")
    col = lax.axis_index("col")
    n_all = n_row * n_col
    me = row * n_col + col
    tile_rows, depth, tile_cols = x_s.shape
    rank = a_f.shape[1]
    own_a = a_in.shape[0]
    own_b = b_in.shape[0]
    chunk = st_c.shape[1]
    groups = rank // LANES

    load_x = pltpu.make_async_copy(tensor, x_s, load_sem.at[0])
    load_x.start()
    load_k = pltpu.make_async_copy(kind.at[0, pl.ds(0, 8)], kind_s, load_sem.at[1])
    load_k.start()

    barrier = pltpu.get_barrier_semaphore()

    def device(d):
        return {"row": lax.div(d, n_col), "col": lax.rem(d, n_col)}

    def greet(k, carry):
        pl.semaphore_signal(
            barrier, inc=1, device_id=device(lax.rem(me + k, n_all)),
            device_id_type=pl.DeviceIdType.MESH,
        )
        return carry

    lax.fori_loop(1, n_all, greet, 0)

    kinds = {
        "a": (n_col, col, lambda d: {"col": d}, 0),
        "b": (n_row, row, lambda d: {"row": d}, 1),
        "c": (n_all, me, device, 2),
    }

    def copy(src, dst, what, slot, target):
        return pltpu.make_async_remote_copy(
            src_ref=src, dst_ref=dst, send_sem=sends.at[slot], recv_sem=recvs.at[slot],
            device_id=kinds[what][2](target), device_id_type=pl.DeviceIdType.MESH,
        )

    def slot_of(what, it, phase):
        return (kinds[what][3] * 2 + phase) * (ITERS + 1) + it

    def send_all(what, it, phase, src, dst):
        n, mine, _, _ = kinds[what]

        def body(k, carry):
            peer = lax.rem(mine + k, n)
            source = src.at[it, mine] if phase == 0 else src.at[it, peer]
            copy(source, dst.at[it, mine], what, slot_of(what, it, phase), peer).start()
            return carry

        lax.fori_loop(1, n, body, 0)

    def whole(what, it, phase, src, dst):
        n, mine, _, _ = kinds[what]
        part = pl.ds(0, n - 1)
        return copy(
            src.at[it, part], dst.at[it, part], what, slot_of(what, it, phase),
            lax.rem(mine + 1, n),
        )

    started = []

    def start(what, it, phase, src, dst):
        send_all(what, it, phase, src, dst)
        started.append((what, it, phase, src, dst))

    for i, ref in enumerate((c_in, mc_in, vc_in)):
        for d in range(n_all):
            g, h = d // groups, d % groups
            split[i, d] = ref[g * chunk : (g + 1) * chunk, h * LANES : (h + 1) * LANES]

    a = a_in[...]
    b = b_in[...]
    st_a[0], st_a[1], st_a[2] = a, ma_in[...], va_in[...]
    st_b[0], st_b[1], st_b[2] = b, mb_in[...], vb_in[...]
    st_c[0], st_c[1], st_c[2] = split[0, me], split[1, me], split[2, me]
    ag_a[0, col] = a.astype(BF16)
    ag_b[0, row] = b.astype(BF16)
    c_f[...] = c_in[...].astype(BF16).astype(F32)

    pl.semaphore_wait(barrier, n_all - 1)
    start("b", 0, 0, ag_b, ag_b)
    start("a", 0, 0, ag_a, ag_a)
    load_x.wait()
    load_k.wait()

    spread = learn_rate * ITERS
    for it in range(ITERS):
        whole("a", it, 0, ag_a, ag_a).wait_recv()
        whole("b", it, 0, ag_b, ag_b).wait_recv()
        if it > 0:
            whole("c", it, 0, ag_c, ag_c).wait_recv()
            for d in range(n_all):
                g, h = d // groups, d % groups
                c_f[g * chunk : (g + 1) * chunk, h * LANES : (h + 1) * LANES] = (
                    ag_c[it, d].astype(BF16).astype(F32)
                )
        a_f[...] = ag_a[it].reshape(tile_rows, rank).astype(F32)
        bt[...] = ag_b[it].reshape(tile_cols, rank).T
        gb[...] = jnp.zeros_like(gb)
        gc[...] = jnp.zeros_like(gc)

        def block(s, carry):
            at = pl.ds(pl.multiple_of(s * BLOCK, BLOCK), BLOCK)
            a8 = a_f[at, :]
            c3 = c_f[...]
            p = (a8[:, None, :] * c3[None]).astype(BF16).reshape(BLOCK * depth, rank)
            m = jnp.dot(p, bt[...], preferred_element_type=F32)
            x = x_s[at].reshape(BLOCK * depth, tile_cols).astype(F32)
            huber = jnp.clip(m - x, -1.0, 1.0)
            logit = 0.5 * jnp.tanh(0.5 * m) + jnp.where(x > 0, -0.5, 0.5)
            is_logit = jnp.broadcast_to(kind_s[0:1, :], m.shape) == 1
            y = jnp.where(is_logit, logit, huber).astype(BF16)
            z = jnp.dot(
                y, ag_b[it].reshape(tile_cols, rank), preferred_element_type=F32
            ).reshape(BLOCK, depth, rank)
            ga[at, :] = jnp.sum(z * c3[None], axis=1) * scales[0]
            gc[...] += jnp.sum(z * a8[:, None, :], axis=0)
            gb[...] += lax.dot_general(
                y, p, (((0,), (0,)), ((), ())), preferred_element_type=F32
            )
            return carry

        lax.fori_loop(0, tile_rows // BLOCK, block, 0)

        gb[...] = gb[...] * scales[1]
        gs_b[it] = gb[...].astype(BF16).reshape(n_row, own_b, rank)
        start("b", it, 1, gs_b, rs_b)
        for d in range(n_all):
            g, h = d // groups, d % groups
            gs_c[it, d] = (
                gc[g * chunk : (g + 1) * chunk, h * LANES : (h + 1) * LANES] * scales[2]
            )
        start("c", it, 1, gs_c, rs_c)
        gs_a[it] = ga[...].astype(BF16).reshape(n_col, own_a, rank)
        start("a", it, 1, gs_a, rs_a)
        rs_c[it, me] = gs_c[it, me]

        counter = STEP + it + 1
        last = it == ITERS - 1

        def apply(state, grad):
            f, m, v = adam_step(state[0], state[1], state[2], grad, counter)
            state[0], state[1], state[2] = f, m, v
            return f

        whole("c", it, 1, gs_c, rs_c).wait_recv()
        c = apply(st_c, jnp.sum(rs_c[it], axis=0))
        ag_c[it + 1, me] = (split[0, me] - c) / spread if last else c
        start("c", it + 1, 0, ag_c, ag_c)

        whole("b", it, 1, gs_b, rs_b).wait_recv()
        grad = gb[pl.ds(pl.multiple_of(row * own_b, own_b), own_b), :]
        for k in range(1, n_row):
            grad = grad + rs_b[it, lax.rem(row + k, n_row)].astype(F32)
        b = apply(st_b, grad)
        if last:
            ob[...] = (b_in[...] - b) / spread
        else:
            ag_b[it + 1, row] = b.astype(BF16)
            start("b", it + 1, 0, ag_b, ag_b)

        whole("a", it, 1, gs_a, rs_a).wait_recv()
        grad = ga[pl.ds(pl.multiple_of(col * own_a, own_a), own_a), :]
        for k in range(1, n_col):
            grad = grad + rs_a[it, lax.rem(col + k, n_col)].astype(F32)
        a = apply(st_a, grad)
        if last:
            oa[...] = (a_in[...] - a) / spread
        else:
            ag_a[it + 1, col] = a.astype(BF16)
            start("a", it + 1, 0, ag_a, ag_a)

    whole("c", ITERS, 0, ag_c, ag_c).wait_recv()
    for d in range(n_all):
        g, h = d // groups, d % groups
        oc[g * chunk : (g + 1) * chunk, h * LANES : (h + 1) * LANES] = ag_c[ITERS, d]
    for args in started:
        whole(*args).wait_send()


def shards(tensor, loss_kind, a, b, c, ma, va, mb, vb, mc, vc):
    tile_rows, depth, tile_cols = tensor.shape
    rank = a.shape[1]
    n_row = lax.axis_size("row")
    n_col = lax.axis_size("col")
    n_all = n_row * n_col
    full_rows = tile_rows * n_row
    full_cols = tile_cols * n_col
    scales = (
        1.0 / math.sqrt(full_cols * depth),
        1.0 / math.sqrt(full_rows * depth),
        1.0 / math.sqrt(full_rows * full_cols),
    )
    chunk = depth * rank // (n_all * LANES)
    own_a, own_b = a.shape[0], b.shape[0]
    vmem = pl.BlockSpec(memory_space=pltpu.VMEM)
    hbm = pl.BlockSpec(memory_space=pl.ANY)
    slots = 6 * (ITERS + 1)
    return pl.pallas_call(
        functools.partial(kernel, n_row, n_col, scales),
        out_shape=tuple(jax.ShapeDtypeStruct(f.shape, F32) for f in (a, b, c)),
        in_specs=[hbm] * 2 + [vmem] * 9,
        out_specs=[vmem] * 3,
        scratch_shapes=[
            pltpu.VMEM(tensor.shape, tensor.dtype),
            pltpu.VMEM((8, tile_cols), jnp.int32),
            pltpu.VMEM((ITERS, n_col, own_a, rank), BF16),
            pltpu.VMEM((ITERS, n_row, own_b, rank), BF16),
            pltpu.VMEM((ITERS + 1, n_all, chunk, LANES), F32),
            pltpu.VMEM((ITERS, n_col, own_a, rank), BF16),
            pltpu.VMEM((ITERS, n_row, own_b, rank), BF16),
            pltpu.VMEM((ITERS, n_all, chunk, LANES), F32),
            pltpu.VMEM((ITERS, n_col, own_a, rank), BF16),
            pltpu.VMEM((ITERS, n_row, own_b, rank), BF16),
            pltpu.VMEM((ITERS, n_all, chunk, LANES), F32),
            pltpu.VMEM((tile_rows, rank), F32),
            pltpu.VMEM((rank, tile_cols), BF16),
            pltpu.VMEM((depth, rank), F32),
            pltpu.VMEM((tile_rows, rank), F32),
            pltpu.VMEM((tile_cols, rank), F32),
            pltpu.VMEM((depth, rank), F32),
            pltpu.VMEM((3, own_a, rank), F32),
            pltpu.VMEM((3, own_b, rank), F32),
            pltpu.VMEM((3, chunk, LANES), F32),
            pltpu.VMEM((3, n_all, chunk, LANES), F32),
            pltpu.SemaphoreType.DMA((2,)),
            pltpu.SemaphoreType.DMA((slots,)),
            pltpu.SemaphoreType.DMA((slots,)),
        ],
        compiler_params=pltpu.CompilerParams(
            collective_id=0, has_side_effects=True, vmem_limit_bytes=60 * 1024 * 1024
        ),
    )(tensor, loss_kind, a, b, c, ma, va, mb, vb, mc, vc)


def solution(mesh):
    in_specs = (
        P("row", None, "col"),
        P("row", None, "col"),
        P(("row", "col"), None),
        P(("col", "row"), None),
        P(),
        P(("row", "col"), None),
        P(("row", "col"), None),
        P(("col", "row"), None),
        P(("col", "row"), None),
        P(),
        P(),
    )
    out_specs = (P(("row", "col"), None), P(("col", "row"), None), P())
    return jax.shard_map(shards, mesh=mesh, in_specs=in_specs, out_specs=out_specs, check_vma=False)
```

```python
import functools
import math

import jax
import jax.numpy as jnp
from jax import lax
from jax.experimental import pallas as pl
from jax.experimental.pallas import tpu as pltpu
from jax.sharding import PartitionSpec as P

ITERS = 2
STEP = 10
BLOCK = 32
LANES = 128

learn_rate = 0.05
beta_one = 0.8
beta_two = 0.95
adam_eps = 1e-08

F32 = jnp.float32
BF16 = jnp.bfloat16


def adam_step(param, first, second, grad, counter):
    first = beta_one * first + (1.0 - beta_one) * grad
    second = beta_two * second + (1.0 - beta_two) * grad * grad
    corr_one = 1.0 - beta_one**counter
    corr_two = 1.0 - beta_two**counter
    param = param - learn_rate * (first / corr_one) / (jnp.sqrt(second / corr_two) + adam_eps)
    return (param, first, second)


def kernel(
    n_row, n_col, scales,
    tensor, kind, a_in, b_in, c_in, ma_in, va_in, mb_in, vb_in, mc_in, vc_in,
    oa, ob, oc,
    x_s, kind_s, ag_a, ag_b, ag_c, gs_a, gs_b, gs_c, rs_a, rs_b, rs_c,
    a_f, bt, c_f, ga, gb, gc, st_a, st_b, st_c, split,
    load_sem, sends, recvs,
):
    row = lax.axis_index("row")
    col = lax.axis_index("col")
    n_all = n_row * n_col
    me = row * n_col + col
    tile_rows, depth, tile_cols = x_s.shape
    rank = a_f.shape[1]
    own_a = a_in.shape[0]
    own_b = b_in.shape[0]
    step_rows = min(BLOCK, own_a)
    chunk = st_c.shape[1]
    groups = rank // LANES

    load_x = pltpu.make_async_copy(tensor, x_s, load_sem.at[0])
    load_x.start()
    load_k = pltpu.make_async_copy(kind.at[0, pl.ds(0, 8)], kind_s, load_sem.at[1])
    load_k.start()

    barrier = pltpu.get_barrier_semaphore()

    def device(d):
        return {"row": lax.div(d, n_col), "col": lax.rem(d, n_col)}

    def greet(k, carry):
        pl.semaphore_signal(
            barrier, inc=1, device_id=device(lax.rem(me + k, n_all)),
            device_id_type=pl.DeviceIdType.MESH,
        )
        return carry

    lax.fori_loop(1, n_all, greet, 0)

    kinds = {
        "a": (n_col, col, lambda d: {"col": d}, 0),
        "b": (n_row, row, lambda d: {"row": d}, 1),
        "c": (n_all, me, device, 2),
    }

    def copy(src, dst, what, slot, target):
        return pltpu.make_async_remote_copy(
            src_ref=src, dst_ref=dst, send_sem=sends.at[slot], recv_sem=recvs.at[slot],
            device_id=kinds[what][2](target), device_id_type=pl.DeviceIdType.MESH,
        )

    def slot_of(what, it, phase):
        return (kinds[what][3] * 2 + phase) * (ITERS + 1) + it

    def send_all(what, it, phase, src, dst):
        n, mine, _, _ = kinds[what]

        def body(k, carry):
            peer = lax.rem(mine + k, n)
            source = src.at[it, mine] if phase == 0 else src.at[it, peer]
            copy(source, dst.at[it, mine], what, slot_of(what, it, phase), peer).start()
            return carry

        lax.fori_loop(1, n, body, 0)

    def whole(what, it, phase, src, dst):
        n, mine, _, _ = kinds[what]
        part = pl.ds(0, n - 1)
        return copy(
            src.at[it, part], dst.at[it, part], what, slot_of(what, it, phase),
            lax.rem(mine + 1, n),
        )

    started = []

    def start(what, it, phase, src, dst):
        send_all(what, it, phase, src, dst)
        started.append((what, it, phase, src, dst))

    for i, ref in enumerate((c_in, mc_in, vc_in)):
        for d in range(n_all):
            g, h = d // groups, d % groups
            split[i, d] = ref[g * chunk : (g + 1) * chunk, h * LANES : (h + 1) * LANES]

    a = a_in[...]
    b = b_in[...]
    st_a[0], st_a[1], st_a[2] = a, ma_in[...], va_in[...]
    st_b[0], st_b[1], st_b[2] = b, mb_in[...], vb_in[...]
    st_c[0], st_c[1], st_c[2] = split[0, me], split[1, me], split[2, me]
    ag_a[0, col] = a.astype(BF16)
    ag_b[0, row] = b.astype(BF16)
    c_f[...] = c_in[...].astype(BF16).astype(F32)

    pl.semaphore_wait(barrier, n_all - 1)
    start("b", 0, 0, ag_b, ag_b)
    start("a", 0, 0, ag_a, ag_a)
    load_x.wait()
    load_k.wait()

    spread = learn_rate * ITERS
    for it in range(ITERS):
        whole("a", it, 0, ag_a, ag_a).wait_recv()
        whole("b", it, 0, ag_b, ag_b).wait_recv()
        if it > 0:
            whole("c", it, 0, ag_c, ag_c).wait_recv()
            for d in range(n_all):
                g, h = d // groups, d % groups
                c_f[g * chunk : (g + 1) * chunk, h * LANES : (h + 1) * LANES] = (
                    ag_c[it, d].astype(BF16).astype(F32)
                )
        a_f[...] = ag_a[it].reshape(tile_rows, rank).astype(F32)
        bt[...] = ag_b[it].reshape(tile_cols, rank).T
        gb[...] = jnp.zeros_like(gb)
        gc[...] = jnp.zeros_like(gc)

        def owner(t, carry):
            q = lax.rem(col + 1 + t, n_col)
            base = pl.multiple_of(q * own_a, own_a)

            def block(s, carry):
                at = pl.ds(pl.multiple_of(base + s * step_rows, step_rows), step_rows)
                a8 = a_f[at, :]
                c3 = c_f[...]
                p = (a8[:, None, :] * c3[None]).astype(BF16).reshape(step_rows * depth, rank)
                m = jnp.dot(p, bt[...], preferred_element_type=F32)
                x = x_s[at].reshape(step_rows * depth, tile_cols).astype(F32)
                huber = jnp.clip(m - x, -1.0, 1.0)
                logit = 0.5 * jnp.tanh(0.5 * m) + jnp.where(x > 0, -0.5, 0.5)
                is_logit = jnp.broadcast_to(kind_s[0:1, :], m.shape) == 1
                y = jnp.where(is_logit, logit, huber).astype(BF16)
                z = jnp.dot(
                    y, ag_b[it].reshape(tile_cols, rank), preferred_element_type=F32
                ).reshape(step_rows, depth, rank)
                ga[at, :] = jnp.sum(z * c3[None], axis=1) * scales[0]
                gc[...] += jnp.sum(z * a8[:, None, :], axis=0)
                gb[...] += lax.dot_general(
                    y, p, (((0,), (0,)), ((), ())), preferred_element_type=F32
                )
                return carry

            lax.fori_loop(0, own_a // step_rows, block, 0)
            gs_a[it, q] = ga[pl.ds(base, own_a), :].astype(BF16)

            @pl.when(t < n_col - 1)
            def _():
                copy(gs_a.at[it, q], rs_a.at[it, col], "a", slot_of("a", it, 1), q).start()

            return carry

        lax.fori_loop(0, n_col, owner, 0)
        started.append(("a", it, 1, gs_a, rs_a))

        gb[...] = gb[...] * scales[1]
        gs_b[it] = gb[...].astype(BF16).reshape(n_row, own_b, rank)
        start("b", it, 1, gs_b, rs_b)
        for d in range(n_all):
            g, h = d // groups, d % groups
            gs_c[it, d] = (
                gc[g * chunk : (g + 1) * chunk, h * LANES : (h + 1) * LANES] * scales[2]
            ).astype(BF16)
        start("c", it, 1, gs_c, rs_c)
        rs_c[it, me] = gs_c[it, me]

        counter = STEP + it + 1
        last = it == ITERS - 1

        def apply(state, grad):
            f, m, v = adam_step(state[0], state[1], state[2], grad, counter)
            state[0], state[1], state[2] = f, m, v
            return f

        whole("a", it, 1, gs_a, rs_a).wait_recv()
        grad = ga[pl.ds(pl.multiple_of(col * own_a, own_a), own_a), :]
        for k in range(1, n_col):
            grad = grad + rs_a[it, lax.rem(col + k, n_col)].astype(F32)
        a = apply(st_a, grad)
        if last:
            oa[...] = (a_in[...] - a) / spread
        else:
            ag_a[it + 1, col] = a.astype(BF16)
            start("a", it + 1, 0, ag_a, ag_a)

        whole("c", it, 1, gs_c, rs_c).wait_recv()
        c = apply(st_c, jnp.sum(rs_c[it].astype(F32), axis=0))
        ag_c[it + 1, me] = (split[0, me] - c) / spread if last else c
        start("c", it + 1, 0, ag_c, ag_c)

        whole("b", it, 1, gs_b, rs_b).wait_recv()
        grad = gb[pl.ds(pl.multiple_of(row * own_b, own_b), own_b), :]
        for k in range(1, n_row):
            grad = grad + rs_b[it, lax.rem(row + k, n_row)].astype(F32)
        b = apply(st_b, grad)
        if last:
            ob[...] = (b_in[...] - b) / spread
        else:
            ag_b[it + 1, row] = b.astype(BF16)
            start("b", it + 1, 0, ag_b, ag_b)

    whole("c", ITERS, 0, ag_c, ag_c).wait_recv()
    for d in range(n_all):
        g, h = d // groups, d % groups
        oc[g * chunk : (g + 1) * chunk, h * LANES : (h + 1) * LANES] = ag_c[ITERS, d]
    for args in started:
        whole(*args).wait_send()


def hand_on(a, b, c, oa, ob, oc):
    oa[...] = a[...]
    ob[...] = b[...]
    oc[...] = c[...]


def shards(tensor, loss_kind, a, b, c, ma, va, mb, vb, mc, vc):
    tile_rows, depth, tile_cols = tensor.shape
    rank = a.shape[1]
    n_row = lax.axis_size("row")
    n_col = lax.axis_size("col")
    n_all = n_row * n_col
    full_rows = tile_rows * n_row
    full_cols = tile_cols * n_col
    scales = (
        1.0 / math.sqrt(full_cols * depth),
        1.0 / math.sqrt(full_rows * depth),
        1.0 / math.sqrt(full_rows * full_cols),
    )
    chunk = depth * rank // (n_all * LANES)
    own_a, own_b = a.shape[0], b.shape[0]
    vmem = pl.BlockSpec(memory_space=pltpu.VMEM)
    hbm = pl.BlockSpec(memory_space=pl.ANY)
    slots = 6 * (ITERS + 1)
    outs = pl.pallas_call(
        functools.partial(kernel, n_row, n_col, scales),
        out_shape=tuple(jax.ShapeDtypeStruct(f.shape, F32) for f in (a, b, c)),
        in_specs=[hbm] * 2 + [vmem] * 9,
        out_specs=[vmem] * 3,
        scratch_shapes=[
            pltpu.VMEM(tensor.shape, tensor.dtype),
            pltpu.VMEM((8, tile_cols), jnp.int32),
            pltpu.VMEM((ITERS, n_col, own_a, rank), BF16),
            pltpu.VMEM((ITERS, n_row, own_b, rank), BF16),
            pltpu.VMEM((ITERS + 1, n_all, chunk, LANES), F32),
            pltpu.VMEM((ITERS, n_col, own_a, rank), BF16),
            pltpu.VMEM((ITERS, n_row, own_b, rank), BF16),
            pltpu.VMEM((ITERS, n_all, chunk, LANES), BF16),
            pltpu.VMEM((ITERS, n_col, own_a, rank), BF16),
            pltpu.VMEM((ITERS, n_row, own_b, rank), BF16),
            pltpu.VMEM((ITERS, n_all, chunk, LANES), BF16),
            pltpu.VMEM((tile_rows, rank), F32),
            pltpu.VMEM((rank, tile_cols), BF16),
            pltpu.VMEM((depth, rank), F32),
            pltpu.VMEM((tile_rows, rank), F32),
            pltpu.VMEM((tile_cols, rank), F32),
            pltpu.VMEM((depth, rank), F32),
            pltpu.VMEM((3, own_a, rank), F32),
            pltpu.VMEM((3, own_b, rank), F32),
            pltpu.VMEM((3, chunk, LANES), F32),
            pltpu.VMEM((3, n_all, chunk, LANES), F32),
            pltpu.SemaphoreType.DMA((2,)),
            pltpu.SemaphoreType.DMA((slots,)),
            pltpu.SemaphoreType.DMA((slots,)),
        ],
        compiler_params=pltpu.CompilerParams(
            collective_id=0, has_side_effects=True, vmem_limit_bytes=60 * 1024 * 1024
        ),
    )(tensor, loss_kind, a, b, c, ma, va, mb, vb, mc, vc)
    return pl.pallas_call(
        hand_on,
        out_shape=tuple(jax.ShapeDtypeStruct(f.shape, F32) for f in (a, b, c)),
        in_specs=[vmem] * 3,
        out_specs=[vmem] * 3,
    )(*outs)


def solution(mesh):
    in_specs = (
        P("row", None, "col"),
        P("row", None, "col"),
        P(("row", "col"), None),
        P(("col", "row"), None),
        P(),
        P(("row", "col"), None),
        P(("row", "col"), None),
        P(("col", "row"), None),
        P(("col", "row"), None),
        P(),
        P(),
    )
    out_specs = (P(("row", "col"), None), P(("col", "row"), None), P())
    return jax.shard_map(shards, mesh=mesh, in_specs=in_specs, out_specs=out_specs, check_vma=False)
```

```python
import functools
import math

import jax
import jax.numpy as jnp
from jax import lax
from jax.experimental import pallas as pl
from jax.experimental.pallas import tpu as pltpu
from jax.sharding import PartitionSpec as P

ITERS = 2
STEP = 10
BLOCK = 32
LANES = 128

learn_rate = 0.05
beta_one = 0.8
beta_two = 0.95
adam_eps = 1e-08

F32 = jnp.float32
BF16 = jnp.bfloat16


def adam_step(param, first, second, grad, counter):
    first = beta_one * first + (1.0 - beta_one) * grad
    second = beta_two * second + (1.0 - beta_two) * grad * grad
    corr_one = 1.0 - beta_one**counter
    corr_two = 1.0 - beta_two**counter
    param = param - learn_rate * (first / corr_one) / (jnp.sqrt(second / corr_two) + adam_eps)
    return (param, first, second)


def kernel(
    n_row, n_col, scales,
    tensor, kind, a_hbm, b_hbm, c_hbm, ma_hbm, va_hbm, mb_hbm, vb_hbm, mc_hbm, vc_hbm,
    oa, ob, oc,
    x_s, kind_s, ag_a, ag_b, ag_c, gs_a, gs_b, gs_c, rs_a, rs_b, rs_c,
    a_f, bt, c_f, ga, gb, gc, st_a, st_b, st_c, split, p_s, y_s,
    a_in, b_in, c_in, ma_in, va_in, mb_in, vb_in, mc_in, vc_in,
    load_sem, sends, recvs,
):
    row = lax.axis_index("row")
    col = lax.axis_index("col")
    n_all = n_row * n_col
    me = row * n_col + col
    tile_rows, depth, tile_cols = x_s.shape
    rank = a_f.shape[1]
    own_a = a_in.shape[0]
    own_b = b_in.shape[0]
    step_rows = min(BLOCK, own_a)
    second_rows = BLOCK * depth
    chunk = st_c.shape[1]
    groups = rank // LANES

    load_x = pltpu.make_async_copy(tensor, x_s, load_sem.at[0])
    load_k = pltpu.make_async_copy(kind.at[0, pl.ds(0, 8)], kind_s, load_sem.at[1])

    pairs = (
        (a_hbm, a_in), (b_hbm, b_in), (c_hbm, c_in), (ma_hbm, ma_in), (va_hbm, va_in),
        (mb_hbm, mb_in), (vb_hbm, vb_in), (mc_hbm, mc_in), (vc_hbm, vc_in),
    )
    loads = [
        pltpu.make_async_copy(src, dst, load_sem.at[2 + i]) for i, (src, dst) in enumerate(pairs)
    ]
    for load in loads:
        load.start()
    load_k.start()
    load_x.start()

    barrier = pltpu.get_barrier_semaphore()

    def device(d):
        return {"row": lax.div(d, n_col), "col": lax.rem(d, n_col)}

    def greet(k, carry):
        pl.semaphore_signal(
            barrier, inc=1, device_id=device(lax.rem(me + k, n_all)),
            device_id_type=pl.DeviceIdType.MESH,
        )
        return carry

    lax.fori_loop(1, n_all, greet, 0)

    kinds = {
        "a": (n_col, col, lambda d: {"col": d}, 0),
        "b": (n_row, row, lambda d: {"row": d}, 1),
        "c": (n_all, me, device, 2),
    }

    def copy(src, dst, what, slot, target):
        return pltpu.make_async_remote_copy(
            src_ref=src, dst_ref=dst, send_sem=sends.at[slot], recv_sem=recvs.at[slot],
            device_id=kinds[what][2](target), device_id_type=pl.DeviceIdType.MESH,
        )

    def slot_of(what, it, phase):
        return (kinds[what][3] * 2 + phase) * (ITERS + 1) + it

    def send_all(what, it, phase, src, dst):
        n, mine, _, _ = kinds[what]

        def body(k, carry):
            peer = lax.rem(mine + k, n)
            source = src.at[it, mine] if phase == 0 else src.at[it, peer]
            copy(source, dst.at[it, mine], what, slot_of(what, it, phase), peer).start()
            return carry

        lax.fori_loop(1, n, body, 0)

    def whole(what, it, phase, src, dst):
        n, mine, _, _ = kinds[what]
        part = pl.ds(0, n - 1)
        return copy(
            src.at[it, part], dst.at[it, part], what, slot_of(what, it, phase),
            lax.rem(mine + 1, n),
        )

    started = []

    def start(what, it, phase, src, dst):
        send_all(what, it, phase, src, dst)
        started.append((what, it, phase, src, dst))

    for load in loads:
        load.wait()
    for i, ref in enumerate((c_in, mc_in, vc_in)):
        for d in range(n_all):
            g, h = d // groups, d % groups
            split[i, d] = ref[g * chunk : (g + 1) * chunk, h * LANES : (h + 1) * LANES]

    a = a_in[...]
    b = b_in[...]
    st_a[0], st_a[1], st_a[2] = a, ma_in[...], va_in[...]
    st_b[0], st_b[1], st_b[2] = b, mb_in[...], vb_in[...]
    st_c[0], st_c[1], st_c[2] = split[0, me], split[1, me], split[2, me]
    ag_a[0, col] = a.astype(BF16)
    ag_b[0, row] = b.astype(BF16)
    c_f[...] = c_in[...].astype(BF16).astype(F32)

    pl.semaphore_wait(barrier, n_all - 1)
    start("b", 0, 0, ag_b, ag_b)
    start("a", 0, 0, ag_a, ag_a)
    load_x.wait()
    load_k.wait()

    spread = learn_rate * ITERS
    for it in range(ITERS):
        whole("a", it, 0, ag_a, ag_a).wait_recv()
        whole("b", it, 0, ag_b, ag_b).wait_recv()
        if it > 0:
            whole("c", it, 0, ag_c, ag_c).wait_recv()
            for d in range(n_all):
                g, h = d // groups, d % groups
                c_f[g * chunk : (g + 1) * chunk, h * LANES : (h + 1) * LANES] = (
                    ag_c[it, d].astype(BF16).astype(F32)
                )
        a_f[...] = ag_a[it].reshape(tile_rows, rank).astype(F32)
        bt[...] = ag_b[it].reshape(tile_cols, rank).T
        gb[...] = jnp.zeros_like(gb)
        gc[...] = jnp.zeros_like(gc)

        def owner(t, carry):
            q = lax.rem(col + 1 + t, n_col)
            base = pl.multiple_of(q * own_a, own_a)

            def block(s, carry):
                at = pl.ds(pl.multiple_of(base + s * step_rows, step_rows), step_rows)
                a8 = a_f[at, :]
                c3 = c_f[...]
                p = (a8[:, None, :] * c3[None]).astype(BF16).reshape(step_rows * depth, rank)
                span = pl.ds(
                    pl.multiple_of((base + s * step_rows) * depth, step_rows * depth), step_rows * depth
                )
                p_s[span, :] = p
                m = jnp.dot(p, bt[...], preferred_element_type=F32)
                x = x_s[at].reshape(step_rows * depth, tile_cols).astype(F32)
                huber = jnp.clip(m - x, -1.0, 1.0)
                logit = 0.5 * jnp.tanh(0.5 * m) + jnp.where(x > 0, -0.5, 0.5)
                is_logit = jnp.broadcast_to(kind_s[0:1, :], m.shape) == 1
                y = jnp.where(is_logit, logit, huber).astype(BF16)
                z = jnp.dot(
                    y, ag_b[it].reshape(tile_cols, rank), preferred_element_type=F32
                ).reshape(step_rows, depth, rank)
                ga[at, :] = jnp.sum(z * c3[None], axis=1) * scales[0]
                gc[...] += jnp.sum(z * a8[:, None, :], axis=0)
                y_s[span, :] = y
                return carry

            lax.fori_loop(0, own_a // step_rows, block, 0)
            gs_a[it, q] = ga[pl.ds(base, own_a), :].astype(BF16)

            @pl.when(t < n_col - 1)
            def _():
                copy(gs_a.at[it, q], rs_a.at[it, col], "a", slot_of("a", it, 1), q).start()

            return carry

        lax.fori_loop(0, n_col, owner, 0)
        started.append(("a", it, 1, gs_a, rs_a))

        for d in range(n_all):
            g, h = d // groups, d % groups
            gs_c[it, d] = (
                gc[g * chunk : (g + 1) * chunk, h * LANES : (h + 1) * LANES] * scales[2]
            ).astype(BF16)
        start("c", it, 1, gs_c, rs_c)
        rs_c[it, me] = gs_c[it, me]

        def second(s, carry):
            span = pl.ds(pl.multiple_of(s * second_rows, second_rows), second_rows)
            gb[...] += lax.dot_general(
                y_s[span, :], p_s[span, :], (((0,), (0,)), ((), ())), preferred_element_type=F32
            )
            return carry

        lax.fori_loop(0, tile_rows * depth // second_rows, second, 0)
        gb[...] = gb[...] * scales[1]
        gs_b[it] = gb[...].astype(BF16).reshape(n_row, own_b, rank)
        start("b", it, 1, gs_b, rs_b)

        counter = STEP + it + 1
        last = it == ITERS - 1

        def apply(state, grad):
            f, m, v = adam_step(state[0], state[1], state[2], grad, counter)
            state[0], state[1], state[2] = f, m, v
            return f

        whole("a", it, 1, gs_a, rs_a).wait_recv()
        grad = ga[pl.ds(pl.multiple_of(col * own_a, own_a), own_a), :]
        for k in range(1, n_col):
            grad = grad + rs_a[it, lax.rem(col + k, n_col)].astype(F32)
        a = apply(st_a, grad)
        if last:
            oa[...] = (a_in[...] - a) / spread
        else:
            ag_a[it + 1, col] = a.astype(BF16)
            start("a", it + 1, 0, ag_a, ag_a)

        whole("c", it, 1, gs_c, rs_c).wait_recv()
        c = apply(st_c, jnp.sum(rs_c[it].astype(F32), axis=0))
        ag_c[it + 1, me] = (split[0, me] - c) / spread if last else c
        start("c", it + 1, 0, ag_c, ag_c)

        whole("b", it, 1, gs_b, rs_b).wait_recv()
        grad = gb[pl.ds(pl.multiple_of(row * own_b, own_b), own_b), :]
        for k in range(1, n_row):
            grad = grad + rs_b[it, lax.rem(row + k, n_row)].astype(F32)
        b = apply(st_b, grad)
        if last:
            ob[...] = (b_in[...] - b) / spread
        else:
            ag_b[it + 1, row] = b.astype(BF16)
            start("b", it + 1, 0, ag_b, ag_b)

    whole("c", ITERS, 0, ag_c, ag_c).wait_recv()
    for d in range(n_all):
        g, h = d // groups, d % groups
        oc[g * chunk : (g + 1) * chunk, h * LANES : (h + 1) * LANES] = ag_c[ITERS, d]
    for args in started:
        whole(*args).wait_send()


def hand_on(a, b, c, oa, ob, oc):
    oa[...] = a[...]
    ob[...] = b[...]
    oc[...] = c[...]


def shards(tensor, loss_kind, a, b, c, ma, va, mb, vb, mc, vc):
    tile_rows, depth, tile_cols = tensor.shape
    rank = a.shape[1]
    n_row = lax.axis_size("row")
    n_col = lax.axis_size("col")
    n_all = n_row * n_col
    full_rows = tile_rows * n_row
    full_cols = tile_cols * n_col
    scales = (
        1.0 / math.sqrt(full_cols * depth),
        1.0 / math.sqrt(full_rows * depth),
        1.0 / math.sqrt(full_rows * full_cols),
    )
    chunk = depth * rank // (n_all * LANES)
    own_a, own_b = a.shape[0], b.shape[0]
    vmem = pl.BlockSpec(memory_space=pltpu.VMEM)
    hbm = pl.BlockSpec(memory_space=pl.ANY)
    slots = 6 * (ITERS + 1)
    outs = pl.pallas_call(
        functools.partial(kernel, n_row, n_col, scales),
        out_shape=tuple(jax.ShapeDtypeStruct(f.shape, F32) for f in (a, b, c)),
        in_specs=[hbm] * 11,
        out_specs=[vmem] * 3,
        scratch_shapes=[
            pltpu.VMEM(tensor.shape, tensor.dtype),
            pltpu.VMEM((8, tile_cols), jnp.int32),
            pltpu.VMEM((ITERS, n_col, own_a, rank), BF16),
            pltpu.VMEM((ITERS, n_row, own_b, rank), BF16),
            pltpu.VMEM((ITERS + 1, n_all, chunk, LANES), F32),
            pltpu.VMEM((ITERS, n_col, own_a, rank), BF16),
            pltpu.VMEM((ITERS, n_row, own_b, rank), BF16),
            pltpu.VMEM((ITERS, n_all, chunk, LANES), BF16),
            pltpu.VMEM((ITERS, n_col, own_a, rank), BF16),
            pltpu.VMEM((ITERS, n_row, own_b, rank), BF16),
            pltpu.VMEM((ITERS, n_all, chunk, LANES), BF16),
            pltpu.VMEM((tile_rows, rank), F32),
            pltpu.VMEM((rank, tile_cols), BF16),
            pltpu.VMEM((depth, rank), F32),
            pltpu.VMEM((tile_rows, rank), F32),
            pltpu.VMEM((tile_cols, rank), F32),
            pltpu.VMEM((depth, rank), F32),
            pltpu.VMEM((3, own_a, rank), F32),
            pltpu.VMEM((3, own_b, rank), F32),
            pltpu.VMEM((3, chunk, LANES), F32),
            pltpu.VMEM((3, n_all, chunk, LANES), F32),
            pltpu.VMEM((tile_rows * depth, rank), BF16),
            pltpu.VMEM((tile_rows * depth, tile_cols), BF16),
            *[pltpu.VMEM(f.shape, F32) for f in (a, b, c, ma, va, mb, vb, mc, vc)],
            pltpu.SemaphoreType.DMA((11,)),
            pltpu.SemaphoreType.DMA((slots,)),
            pltpu.SemaphoreType.DMA((slots,)),
        ],
        compiler_params=pltpu.CompilerParams(
            collective_id=0, has_side_effects=True, vmem_limit_bytes=60 * 1024 * 1024
        ),
    )(tensor, loss_kind, a, b, c, ma, va, mb, vb, mc, vc)
    return pl.pallas_call(
        hand_on,
        out_shape=tuple(jax.ShapeDtypeStruct(f.shape, F32) for f in (a, b, c)),
        in_specs=[vmem] * 3,
        out_specs=[vmem] * 3,
    )(*outs)


def solution(mesh):
    in_specs = (
        P("row", None, "col"),
        P("row", None, "col"),
        P(("row", "col"), None),
        P(("col", "row"), None),
        P(),
        P(("row", "col"), None),
        P(("row", "col"), None),
        P(("col", "row"), None),
        P(("col", "row"), None),
        P(),
        P(),
    )
    out_specs = (P(("row", "col"), None), P(("col", "row"), None), P())
    return jax.shard_map(shards, mesh=mesh, in_specs=in_specs, out_specs=out_specs, check_vma=False)
```
